32 devices in a mesh: row: 16 (over z, x, core), col: 2 (over y).
Axes of the slice: x: 2, y: 2, z: 4, core: 2. Of those that a mesh axis runs over, the one named last changes fastest.
Arguments:
- ham: bfloat16 [8192, 8192], P('row'), may hold values from -0.2 to 1.7, as said below
- coeff: bfloat16 [8192, 8192], P('row', 'col'), may hold values from -40 to 40, as said below
- tile_mask: int32 [256, 256], P('row'), may hold values from 0 to 1, as said below
- occupation: int32 [16, 8192], replicated, may hold values from 0 to 1, as said below
- orbital_energy: float32 [16], replicated, may hold values from -0.4 to 0.6
- coulomb: float32 [16, 16], replicated, may hold values from 0.005 to 0.04
Outputs:
- correction: float32 [8192, 8192], P('row', 'col')
- stats: float32 [2], replicated
The draws below stay inside these ranges and needn't reach their ends.
Inputs may be any that keep to these rules, and one draw needn't show every extreme that they name: ham is symmetric. coeff is symmetric. tile_mask is symmetric with ones on its diagonal. `occupation`: every column holds exactly 6 ones.
All inputs are finite; a program needn't handle non-finite values.
Results may differ from the reference program's by a relative error of at most 0.0003.
Values may be sent and summed in bfloat16 or wider, within the bound.
A program may use at most 192 MiB of HBM per device.

```python
import math
import jax
import jax.numpy as jnp
from jax import lax

NS = 8192
NORB = 16
NEL = 6
STR_BLOCK = 32


def string_scales(key):
    uniform_part = jax.random.uniform(key, (NS,), jnp.float32)
    position = jnp.arange(NS, dtype=jnp.float32) / NS
    return jnp.exp(uniform_part * math.log(10.0)) * (1.0 + position)


def draw_coeff(key, part):
    key_entries = jax.random.fold_in(key, 11)
    key_scales = jax.random.fold_in(key, 12)
    entries = jax.random.normal(key_entries, (NS, NS), jnp.float32)
    scales = string_scales(key_scales)
    norm_scale = 50.0
    paired = jnp.clip((entries + entries.T) * 0.7071, -4.0, 4.0)
    return (paired * scales[:, None] * scales[None, :] / norm_scale).astype(jnp.bfloat16)


def draw_ham(key, part):
    key_entries = jax.random.fold_in(key, 21)
    key_diagonal = jax.random.fold_in(key, 22)
    entries = jnp.clip(jax.random.normal(key_entries, (NS, NS), jnp.float32), -6.0, 6.0)
    diagonal = jax.random.uniform(key_diagonal, (NS,), jnp.float32, 0.5, 1.5)
    paired = (entries + entries.T) * (0.7071 / math.sqrt(NS))
    return (paired + jnp.diag(diagonal)).astype(jnp.bfloat16)


def draw_tile_mask(key, part):
    block_count = NS // STR_BLOCK
    coin_flips = jax.random.randint(jax.random.fold_in(key, 31), (block_count, block_count), 0, 2, jnp.int32)
    row_index = jnp.arange(block_count, dtype=jnp.int32)[:, None]
    col_index = jnp.arange(block_count, dtype=jnp.int32)[None, :]
    mirrored = jnp.where(row_index <= col_index, coin_flips, coin_flips.T)
    return jnp.where(row_index == col_index, 1, mirrored).astype(jnp.int32)


def draw_occupation(key, part):
    keys_all = jax.random.split(jax.random.fold_in(key, 41), NS)
    orders = jax.vmap(lambda one_key: jax.random.permutation(one_key, NORB))(keys_all)
    return (orders < NEL).astype(jnp.int32).T


def setup_inputs(seed: int = 0) -> dict:
    arg_keys = jax.random.split(jax.random.key(seed), 7)
    return {
        "ham": draw_ham(jax.random.fold_in(arg_keys[6], 71), 0),
        "coeff": draw_coeff(jax.random.fold_in(arg_keys[6], 71), 0),
        "tile_mask": draw_tile_mask(jax.random.fold_in(arg_keys[6], 71), 0),
        "occupation": draw_occupation(jax.random.fold_in(arg_keys[6], 71), 0),
        "orbital_energy": jnp.clip(jax.random.uniform(arg_keys[4], (NORB,), jnp.float32, -0.4, 0.6), -0.4, 0.6),
        "coulomb": jnp.clip(jnp.exp(jax.random.uniform(arg_keys[5], (NORB, NORB), jnp.float32, math.log(0.005), math.log(0.04))), 0.005, 0.04),
    }


def reference(ham, coeff, tile_mask, occupation, orbital_energy, coulomb):
    block_count = tile_mask.shape[0]
    block_size = NS // block_count
    weights = tile_mask.astype(jnp.bfloat16)[:, None, :, None]
    masked = (ham.reshape(block_count, block_size, block_count, block_size) * weights).reshape(NS, NS)
    product = jnp.dot(masked, coeff, preferred_element_type=jnp.float32)
    sigma = product + product.T
    coeff_float = coeff.astype(jnp.float32)
    theta = jnp.sum(coeff_float * sigma) / jnp.sum(coeff_float * coeff_float)
    occ_float = occupation.astype(jnp.float32)
    energy = jnp.dot(orbital_energy, occ_float, precision=lax.Precision.HIGHEST)
    coupling = jnp.dot(jnp.dot(occ_float.T, coulomb, precision=lax.Precision.HIGHEST), occ_float, precision=lax.Precision.HIGHEST)
    diagonal = energy[:, None] + energy[None, :] + coupling
    residual = sigma - theta * coeff_float
    update = residual / jnp.maximum(jnp.abs(diagonal - theta), 1.0)
    squares = jnp.sum(residual * residual)
    spread = jnp.sum(update * update)
    correction = update * lax.rsqrt(spread / (NS * NS) + 1e-06)
    stats = jnp.stack([theta, jnp.sqrt(squares / (NS * NS))])
    return (correction, stats)
```

```python
import functools

import jax
import jax.numpy as jnp
from jax import lax
from jax.experimental import pallas as pl
from jax.experimental.pallas import tpu as pltpu
from jax.sharding import PartitionSpec as P

MESH = pl.DeviceIdType.MESH
HIGH = lax.Precision.HIGHEST


def turn_kernel(
    row_count,
    col_count,
    total,
    p_ref,
    c_ref,
    left_ref,
    right_ref,
    out_ref,
    stats_ref,
    recv,
    relay_a,
    relay_b,
    mine,
    sums,
    own_send,
    recv_sem,
    arrive_a,
    arrive_b,
    relay_send,
    sum_send,
    sum_recv,
):
    row = lax.axis_index("row")
    col = lax.axis_index("col")
    tile = p_ref.shape[0]
    half = tile // 2
    fold = row_count // col_count
    home = lax.div(row, fold)
    place = lax.rem(row, fold)
    count = row_count * col_count
    me = row * col_count + col
    is_home = home == col

    barrier = pltpu.get_barrier_semaphore()

    def greet(d, carry):
        other = lax.rem(me + d, count)
        pl.semaphore_signal(
            barrier,
            inc=1,
            device_id=(lax.div(other, col_count), lax.rem(other, col_count)),
            device_id_type=MESH,
        )
        return carry

    lax.fori_loop(1, count, greet, 0)
    pl.semaphore_wait(barrier, count - 1)

    def columns(s):
        return pl.ds(pl.multiple_of(s * tile, tile), tile)

    def remote(src, dst, send, arrive, to_row, to_col):
        return pltpu.make_async_remote_copy(
            src_ref=src,
            dst_ref=dst,
            send_sem=send,
            recv_sem=arrive,
            device_id=(to_row, to_col),
            device_id_type=MESH,
        )

    def own_copies(k):
        s = lax.rem(place + k, fold)
        upper = p_ref.at[pl.ds(0, half), columns(s)]
        lower = p_ref.at[pl.ds(half, half), columns(s)]
        near = col * fold + s
        slot_a = col - (col > home).astype(jnp.int32)
        slot_b = row - fold * (home > col).astype(jnp.int32)
        direct = (
            remote(upper, recv.at[place, pl.ds(0, half)], own_send.at[k, 0], recv_sem.at[place, 0], near, col),
            remote(lower, recv.at[place, pl.ds(half, half)], own_send.at[k, 1], recv_sem.at[place, 1], near, col),
        )
        return direct, upper, lower, s, near, slot_a, slot_b

    def own_relayed(k):
        _, upper, lower, s, near, slot_a, slot_b = own_copies(k)
        return (
            remote(upper, relay_a.at[slot_a, s], own_send.at[k, 0], arrive_a.at[slot_a, s], row, home),
            remote(lower, relay_b.at[slot_b], own_send.at[k, 1], arrive_b.at[slot_b], near, col),
        )

    def exchange(phase, start):
        def one(d, carry):
            other = lax.rem(me + d, count)
            copy = remote(
                mine.at[phase],
                sums.at[phase, me],
                sum_send.at[phase, d],
                sum_recv.at[phase, me],
                lax.div(other, col_count),
                lax.rem(other, col_count),
            )
            if start:
                copy.start()
            else:
                copy.wait_send()
            return carry

        lax.fori_loop(1, count, one, 0)

    def gather_sums(phase):
        def one(d, carry):
            other = lax.rem(me + d, count)
            remote(
                mine.at[phase],
                sums.at[phase, other],
                sum_send.at[phase, d],
                sum_recv.at[phase, other],
                lax.div(other, col_count),
                lax.rem(other, col_count),
            ).wait_recv()
            return carry

        lax.fori_loop(1, count, one, 0)
        sums[phase, pl.ds(me, 1)] = mine[pl.ds(phase, 1)]
        every = jnp.sum(sums[phase], axis=0)
        return jnp.sum(every[0:8]), jnp.sum(every[8:16])

    def fold_sum(x):
        lanes = x.shape[1] // 128
        out = x[:, 0:128]
        for q in range(1, lanes):
            out = out + x[:, q * 128 : (q + 1) * 128]
        return jnp.sum(out.reshape(x.shape[0] // 8, 8, 128), axis=0)

    step_rows = min(32, tile)

    def early(r, carry):
        rows = pl.ds(pl.multiple_of(r * step_rows, step_rows), step_rows)
        c = c_ref[rows, :].astype(jnp.float32)
        return carry[0] + fold_sum(c * p_ref[rows, :]), carry[1] + fold_sum(c * c)

    zero = jnp.zeros((8, 128), jnp.float32)
    proj, weight = lax.fori_loop(0, tile // step_rows, early, (zero, zero))
    mine[0, 0:8] = proj
    mine[0, 8:16] = weight
    exchange(0, True)

    @pl.when(is_home)
    def _():
        def send(k, carry):
            for copy in own_copies(k)[0]:
                copy.start()
            return carry

        lax.fori_loop(1, fold, send, 0)
        pltpu.make_async_copy(
            p_ref.at[pl.ds(0, half), columns(place)], recv.at[place, pl.ds(0, half)], recv_sem.at[place, 0]
        ).start()
        pltpu.make_async_copy(
            p_ref.at[pl.ds(half, half), columns(place)], recv.at[place, pl.ds(half, half)], recv_sem.at[place, 1]
        ).start()

    @pl.when(jnp.logical_not(is_home))
    def _():
        def send(k, carry):
            for copy in own_relayed(k):
                copy.start()
            return carry

        lax.fori_loop(0, fold, send, 0)

    def relays(t):
        slot = lax.div(t, fold)
        k = lax.rem(t, fold)
        group = slot + (slot >= col).astype(jnp.int32)
        s = lax.rem(place + k, fold)
        far = lax.rem(place - k + fold, fold)
        slot_b = slot * fold + far
        copy_a = remote(
            relay_a.at[slot, s],
            recv.at[place, pl.ds(0, half)],
            relay_send.at[t, 0],
            recv_sem.at[place, 0],
            group * fold + s,
            col,
        )
        copy_b = remote(
            relay_b.at[slot_b],
            recv.at[far, pl.ds(half, half)],
            relay_send.at[t, 1],
            recv_sem.at[far, 1],
            row,
            group,
        )
        return slot, s, slot_b, copy_a, copy_b

    relay_steps = (col_count - 1) * fold

    @pl.when(is_home)
    def _():
        def step(t, carry):
            slot, s, slot_b, copy_a, copy_b = relays(t)
            pltpu.make_async_copy(relay_a.at[slot, s], relay_a.at[slot, s], arrive_a.at[slot, s]).wait()
            copy_a.start()
            pltpu.make_async_copy(relay_b.at[slot_b], relay_b.at[slot_b], arrive_b.at[slot_b]).wait()
            copy_b.start()
            return carry

        lax.fori_loop(0, relay_steps, step, 0)

    proj, weight = gather_sums(0)
    theta = 2.0 * proj / weight

    piece = min(128, tile)

    def finish(k, carry):
        s = lax.rem(place - k + fold, fold)
        upper = recv.at[s, pl.ds(0, half)]
        lower = recv.at[s, pl.ds(half, half)]
        pltpu.make_async_copy(upper, upper, recv_sem.at[s, 0]).wait()
        pltpu.make_async_copy(lower, lower, recv_sem.at[s, 1]).wait()
        cols = columns(s)

        def part(r, carry):
            squares, spread = carry
            rows = pl.ds(pl.multiple_of(r * piece, piece), piece)
            turned = recv[s, :, rows].T
            diagonal = jnp.dot(
                left_ref[rows, :], right_ref[:, cols], precision=HIGH, preferred_element_type=jnp.float32
            )
            sigma = p_ref[rows, cols] + turned
            residual = sigma - theta * c_ref[rows, cols].astype(jnp.float32)
            update = residual / jnp.maximum(jnp.abs(diagonal - theta), 1.0)
            out_ref[rows, cols] = update
            return squares + fold_sum(residual * residual), spread + fold_sum(update * update)

        return lax.fori_loop(0, tile // piece, part, carry)

    squares, spread = lax.fori_loop(0, fold, finish, (zero, zero))
    mine[1, 0:8] = squares
    mine[1, 8:16] = spread
    exchange(1, True)
    squares, spread = gather_sums(1)
    stats_ref[0] = theta
    stats_ref[1] = squares / total
    stats_ref[2] = spread / total

    exchange(0, False)
    exchange(1, False)

    @pl.when(is_home)
    def _():
        def done(k, carry):
            for copy in own_copies(k)[0]:
                copy.wait_send()
            return carry

        lax.fori_loop(1, fold, done, 0)

        def done_relay(t, carry):
            _, _, _, copy_a, copy_b = relays(t)
            copy_a.wait_send()
            copy_b.wait_send()
            return carry

        lax.fori_loop(0, relay_steps, done_relay, 0)

    @pl.when(jnp.logical_not(is_home))
    def _():
        def done(k, carry):
            for copy in own_relayed(k):
                copy.wait_send()
            return carry

        lax.fori_loop(0, fold, done, 0)


def turn_and_finish(product, coeff, left, right, strings):
    tile_rows, tile_cols = product.shape
    row_count = lax.axis_size("row")
    col_count = lax.axis_size("col")
    fold = row_count // col_count
    count = row_count * col_count
    half = tile_rows // 2
    others = max(col_count - 1, 1)
    vmem = pl.BlockSpec(memory_space=pltpu.VMEM)
    dma = pltpu.SemaphoreType.DMA
    return pl.pallas_call(
        functools.partial(turn_kernel, row_count, col_count, float(strings) * float(strings)),
        out_shape=(
            jax.ShapeDtypeStruct((tile_rows, tile_cols), jnp.float32),
            jax.ShapeDtypeStruct((3,), jnp.float32),
        ),
        in_specs=[vmem] * 4,
        out_specs=(vmem, pl.BlockSpec(memory_space=pltpu.SMEM)),
        scratch_shapes=[
            pltpu.VMEM((fold, tile_rows, tile_rows), jnp.float32),
            pltpu.VMEM((others, fold, half, tile_rows), jnp.float32),
            pltpu.VMEM((others * fold, half, tile_rows), jnp.float32),
            pltpu.VMEM((2, 16, 128), jnp.float32),
            pltpu.VMEM((2, count, 16, 128), jnp.float32),
            dma((fold, 2)),
            dma((fold, 2)),
            dma((others, fold)),
            dma((others * fold,)),
            dma((others * fold, 2)),
            dma((2, count)),
            dma((2, count)),
        ],
        compiler_params=pltpu.CompilerParams(
            collective_id=0, has_side_effects=True, vmem_limit_bytes=60 * 1024 * 1024
        ),
        name="turn_and_finish",
    )(product, coeff, left, right)


def body(ham, coeff, tile_mask, occupation, orbital_energy, coulomb):
    tile_rows, strings = ham.shape
    tile_cols = coeff.shape[1]
    mask_cols = tile_mask.shape[1]
    block_size = strings // mask_cols
    mask_rows = tile_rows // block_size
    weights = tile_mask.astype(jnp.bfloat16)[:, None, :, None]
    masked = (ham.reshape(mask_rows, block_size, mask_cols, block_size) * weights).reshape(
        tile_rows, strings
    )
    occ_float = occupation.astype(jnp.float32)
    occ_alpha = lax.dynamic_slice_in_dim(occ_float, lax.axis_index("row") * tile_rows, tile_rows, 1)
    occ_beta = lax.dynamic_slice_in_dim(occ_float, lax.axis_index("col") * tile_cols, tile_cols, 1)
    energy_alpha = jnp.dot(orbital_energy, occ_alpha, precision=HIGH)
    energy_beta = jnp.dot(orbital_energy, occ_beta, precision=HIGH)
    mixed = jnp.dot(occ_alpha.T, coulomb, precision=HIGH)
    orbitals = occupation.shape[0]
    depth = -(-(orbitals + 2) // 128) * 128
    left = jnp.concatenate(
        [mixed, energy_alpha[:, None], jnp.ones((tile_rows, 1)), jnp.zeros((tile_rows, depth - orbitals - 2))],
        axis=1,
    )
    right = jnp.concatenate(
        [occ_beta, jnp.ones((1, tile_cols)), energy_beta[None, :], jnp.zeros((depth - orbitals - 2, tile_cols))],
        axis=0,
    )
    product = jnp.dot(
        masked, lax.all_gather(coeff, "row", axis=0, tiled=True), preferred_element_type=jnp.float32
    )
    update, sums = turn_and_finish(product, coeff, left, right, strings)
    correction = update * lax.rsqrt(sums[2] + 1e-06)
    stats = jnp.stack([sums[0], jnp.sqrt(sums[1])])
    return (correction, stats)


def solution(mesh):
    in_specs = (P("row", None), P("row", "col"), P("row", None), P(), P(), P())
    out_specs = (P("row", "col"), P())
    return jax.shard_map(body, mesh=mesh, in_specs=in_specs, out_specs=out_specs, check_vma=False)
```

```python
import functools

import jax
import jax.numpy as jnp
from jax import lax
from jax.experimental import pallas as pl
from jax.experimental.pallas import tpu as pltpu
from jax.sharding import PartitionSpec as P

MESH = pl.DeviceIdType.MESH
HIGH = lax.Precision.HIGHEST


def turn_kernel(
    row_count,
    col_count,
    total,
    *refs,
):
    chunks = refs[:-21]
    (
        c_ref,
        left_ref,
        right_ref,
        out_ref,
        stats_ref,
        p_ref,
        packed,
        recv,
        relay_a,
        relay_b,
        mine,
        sums,
        load_sem,
        own_send,
        recv_sem,
        arrive_a,
        arrive_b,
        relay_send,
        sum_send,
        sum_recv,
        self_sem,
    ) = refs[-21:]
    row = lax.axis_index("row")
    col = lax.axis_index("col")
    tile = p_ref.shape[0]
    half = tile // 2
    fold = row_count // col_count
    home = lax.div(row, fold)
    place = lax.rem(row, fold)
    count = row_count * col_count
    me = row * col_count + col
    is_home = home == col
    width = p_ref.shape[1] // len(chunks)
    loads = [
        pltpu.make_async_copy(chunk, p_ref.at[:, pl.ds(q * width, width)], load_sem.at[q])
        for q, chunk in enumerate(chunks)
    ]
    for load in loads:
        load.start()

    barrier = pltpu.get_barrier_semaphore()

    def greet(d, carry):
        other = lax.rem(me + d, count)
        pl.semaphore_signal(
            barrier,
            inc=1,
            device_id=(lax.div(other, col_count), lax.rem(other, col_count)),
            device_id_type=MESH,
        )
        return carry

    lax.fori_loop(1, count, greet, 0)
    pl.semaphore_wait(barrier, count - 1)
    for load in loads:
        load.wait()

    def columns(s):
        return pl.ds(pl.multiple_of(s * tile, tile), tile)

    def remote(src, dst, send, arrive, to_row, to_col):
        return pltpu.make_async_remote_copy(
            src_ref=src,
            dst_ref=dst,
            send_sem=send,
            recv_sem=arrive,
            device_id=(to_row, to_col),
            device_id_type=MESH,
        )

    def own_direct(k):
        s = lax.rem(place + k, fold)
        near = col * fold + s
        return [
            remote(packed.at[s, h], recv.at[place, h], own_send.at[s, h], recv_sem.at[place, h], near, col)
            for h in range(2)
        ]

    def own_relayed(k):
        s = lax.rem(place + k, fold)
        near = col * fold + s
        slot_a = col - (col > home).astype(jnp.int32)
        slot_b = row - fold * (home > col).astype(jnp.int32)
        return [
            remote(packed.at[s, 0], relay_a.at[slot_a, s], own_send.at[s, 0], arrive_a.at[slot_a, s], row, home),
            remote(packed.at[s, 1], relay_b.at[slot_b], own_send.at[s, 1], arrive_b.at[slot_b], near, col),
        ]

    def own_local():
        return [pltpu.make_async_copy(packed.at[place, h], recv.at[place, h], self_sem.at[h]) for h in range(2)]

    def pack(k):
        s = lax.rem(place + k, fold)
        cols = columns(s)
        for h in range(2):
            peak = jnp.max(jnp.abs(p_ref[pl.ds(h * half, half), cols]), axis=0, keepdims=True)
            code = jnp.floor(jnp.log2(jnp.maximum(peak, 1e-30)) * 128.0) + 2.0
            grow = jnp.exp2(code * (-1.0 / 128.0)) * 32767.0
            packed[s, h, pl.ds(half, 16)] = jnp.broadcast_to(code, (16, tile)).astype(jnp.int32).astype(jnp.int16)
            rows = min(64, half)
            for r in range(0, half, rows):
                value = p_ref[pl.ds(h * half + r, rows), cols] * grow
                packed[s, h, pl.ds(r, rows)] = jnp.floor(value + 0.5).astype(jnp.int32).astype(jnp.int16)

    def exchange(phase, start):
        def one(d, carry):
            other = lax.rem(me + d, count)
            copy = remote(
                mine.at[phase],
                sums.at[phase, me],
                sum_send.at[phase, d],
                sum_recv.at[phase, me],
                lax.div(other, col_count),
                lax.rem(other, col_count),
            )
            if start:
                copy.start()
            else:
                copy.wait_send()
            return carry

        lax.fori_loop(1, count, one, 0)

    def gather_sums(phase):
        def one(d, carry):
            other = lax.rem(me + d, count)
            remote(
                mine.at[phase],
                sums.at[phase, other],
                sum_send.at[phase, d],
                sum_recv.at[phase, other],
                lax.div(other, col_count),
                lax.rem(other, col_count),
            ).wait_recv()
            return carry

        lax.fori_loop(1, count, one, 0)
        sums[phase, pl.ds(me, 1)] = mine[pl.ds(phase, 1)]
        every = jnp.sum(sums[phase], axis=0)
        return jnp.sum(every[0:8]), jnp.sum(every[8:16])

    def fold_sum(x):
        lanes = x.shape[1] // 128
        out = x[:, 0:128]
        for q in range(1, lanes):
            out = out + x[:, q * 128 : (q + 1) * 128]
        return jnp.sum(out.reshape(x.shape[0] // 8, 8, 128), axis=0)

    step_rows = min(32, tile)

    def early(r, carry):
        rows = pl.ds(pl.multiple_of(r * step_rows, step_rows), step_rows)
        c = c_ref[rows, :].astype(jnp.float32)
        return carry[0] + fold_sum(c * p_ref[rows, :]), carry[1] + fold_sum(c * c)

    zero = jnp.zeros((8, 128), jnp.float32)
    proj, weight = lax.fori_loop(0, tile // step_rows, early, (zero, zero))
    mine[0, 0:8] = proj
    mine[0, 8:16] = weight
    exchange(0, True)

    def launch(k, carry):
        pack(k)

        @pl.when(jnp.logical_not(is_home))
        def _():
            for copy in own_relayed(k):
                copy.start()

        @pl.when(jnp.logical_and(is_home, k > 0))
        def _():
            for copy in own_direct(k):
                copy.start()

        return carry

    lax.fori_loop(0, fold, launch, 0)

    @pl.when(is_home)
    def _():
        for copy in own_local():
            copy.start()
        for copy in own_local():
            copy.wait()

    def relays(t):
        slot = lax.div(t, fold)
        k = lax.rem(t, fold)
        group = slot + (slot >= col).astype(jnp.int32)
        s = lax.rem(place + k, fold)
        far = lax.rem(place - k + fold, fold)
        slot_b = slot * fold + far
        copy_a = remote(
            relay_a.at[slot, s],
            recv.at[place, 0],
            relay_send.at[t, 0],
            recv_sem.at[place, 0],
            group * fold + s,
            col,
        )
        copy_b = remote(
            relay_b.at[slot_b],
            recv.at[far, 1],
            relay_send.at[t, 1],
            recv_sem.at[far, 1],
            row,
            group,
        )
        return slot, s, slot_b, copy_a, copy_b

    relay_steps = (col_count - 1) * fold

    @pl.when(is_home)
    def _():
        def step(t, carry):
            slot, s, slot_b, copy_a, copy_b = relays(t)
            pltpu.make_async_copy(relay_a.at[slot, s], relay_a.at[slot, s], arrive_a.at[slot, s]).wait()
            copy_a.start()
            pltpu.make_async_copy(relay_b.at[slot_b], relay_b.at[slot_b], arrive_b.at[slot_b]).wait()
            copy_b.start()
            return carry

        lax.fori_loop(0, relay_steps, step, 0)

    proj, weight = gather_sums(0)
    theta = 2.0 * proj / weight

    piece = min(128, tile)

    def finish(k, carry):
        s = lax.rem(place - k + fold, fold)

        @pl.when(jnp.logical_not(jnp.logical_and(is_home, k == 0)))
        def _():
            for h in range(2):
                pltpu.make_async_copy(recv.at[s, h], recv.at[s, h], recv_sem.at[s, h]).wait()

        def part(r, carry):
            squares, spread = carry
            rows = pl.ds(pl.multiple_of(r * piece, piece), piece)
            for h in range(2):
                cols = pl.ds(pl.multiple_of(s * tile + h * half, half), half)
                code = recv[s, h, pl.ds(half, 16), rows].astype(jnp.int32).astype(jnp.float32)[0:1]
                shrink = jnp.exp2(code * (1.0 / 128.0)) * (1.0 / 32767.0)
                value = recv[s, h, pl.ds(0, half), rows].astype(jnp.int32).astype(jnp.float32)
                turned = (value * shrink).T
                diagonal = jnp.dot(
                    left_ref[rows, :], right_ref[:, cols], precision=HIGH, preferred_element_type=jnp.float32
                )
                sigma = p_ref[rows, cols] + turned
                residual = sigma - theta * c_ref[rows, cols].astype(jnp.float32)
                update = residual / jnp.maximum(jnp.abs(diagonal - theta), 1.0)
                out_ref[rows, cols] = update
                squares = squares + fold_sum(residual * residual)
                spread = spread + fold_sum(update * update)
            return squares, spread

        return lax.fori_loop(0, tile // piece, part, carry)

    squares, spread = lax.fori_loop(0, fold, finish, (zero, zero))
    mine[1, 0:8] = squares
    mine[1, 8:16] = spread
    exchange(1, True)
    squares, spread = gather_sums(1)
    stats_ref[0] = theta
    stats_ref[1] = squares / total
    stats_ref[2] = spread / total

    exchange(0, False)
    exchange(1, False)

    @pl.when(is_home)
    def _():
        def done(k, carry):
            for copy in own_direct(k):
                copy.wait_send()
            return carry

        lax.fori_loop(1, fold, done, 0)

        def done_relay(t, carry):
            _, _, _, copy_a, copy_b = relays(t)
            copy_a.wait_send()
            copy_b.wait_send()
            return carry

        lax.fori_loop(0, relay_steps, done_relay, 0)

    @pl.when(jnp.logical_not(is_home))
    def _():
        def done(k, carry):
            for copy in own_relayed(k):
                copy.wait_send()
            return carry

        lax.fori_loop(0, fold, done, 0)


def turn_and_finish(products, coeff, left, right, strings):
    tile_rows, tile_cols = coeff.shape
    row_count = lax.axis_size("row")
    col_count = lax.axis_size("col")
    fold = row_count // col_count
    count = row_count * col_count
    tall = tile_rows // 2 + 16
    others = max(col_count - 1, 1)
    vmem = pl.BlockSpec(memory_space=pltpu.VMEM)
    dma = pltpu.SemaphoreType.DMA
    return pl.pallas_call(
        functools.partial(turn_kernel, row_count, col_count, float(strings) * float(strings)),
        out_shape=(
            jax.ShapeDtypeStruct((tile_rows, tile_cols), jnp.float32),
            jax.ShapeDtypeStruct((3,), jnp.float32),
        ),
        in_specs=[pl.BlockSpec(memory_space=pl.ANY)] * len(products) + [vmem] * 3,
        out_specs=(vmem, pl.BlockSpec(memory_space=pltpu.SMEM)),
        scratch_shapes=[
            pltpu.VMEM((tile_rows, tile_cols), jnp.float32),
            pltpu.VMEM((fold, 2, tall, tile_rows), jnp.int16),
            pltpu.VMEM((fold, 2, tall, tile_rows), jnp.int16),
            pltpu.VMEM((others, fold, tall, tile_rows), jnp.int16),
            pltpu.VMEM((others * fold, tall, tile_rows), jnp.int16),
            pltpu.VMEM((2, 16, 128), jnp.float32),
            pltpu.VMEM((2, count, 16, 128), jnp.float32),
            dma((len(products),)),
            dma((fold, 2)),
            dma((fold, 2)),
            dma((others, fold)),
            dma((others * fold,)),
            dma((others * fold, 2)),
            dma((2, count)),
            dma((2, count)),
            dma((2,)),
        ],
        compiler_params=pltpu.CompilerParams(
            collective_id=0, has_side_effects=True, vmem_limit_bytes=60 * 1024 * 1024
        ),
        name="turn_and_finish",
    )(*products, coeff, left, right)


CHUNKS = 2


def body(ham, coeff, tile_mask, occupation, orbital_energy, coulomb):
    tile_rows, strings = ham.shape
    tile_cols = coeff.shape[1]
    mask_cols = tile_mask.shape[1]
    block_size = strings // mask_cols
    mask_rows = tile_rows // block_size
    weights = tile_mask.astype(jnp.bfloat16)[:, None, :, None]
    masked = (ham.reshape(mask_rows, block_size, mask_cols, block_size) * weights).reshape(
        tile_rows, strings
    )
    occ_float = occupation.astype(jnp.float32)
    occ_alpha = lax.dynamic_slice_in_dim(occ_float, lax.axis_index("row") * tile_rows, tile_rows, 1)
    occ_beta = lax.dynamic_slice_in_dim(occ_float, lax.axis_index("col") * tile_cols, tile_cols, 1)
    energy_alpha = jnp.dot(orbital_energy, occ_alpha, precision=HIGH)
    energy_beta = jnp.dot(orbital_energy, occ_beta, precision=HIGH)
    mixed = jnp.dot(occ_alpha.T, coulomb, precision=HIGH)
    orbitals = occupation.shape[0]
    depth = -(-(orbitals + 2) // 128) * 128
    left = jnp.concatenate(
        [mixed, energy_alpha[:, None], jnp.ones((tile_rows, 1)), jnp.zeros((tile_rows, depth - orbitals - 2))],
        axis=1,
    )
    right = jnp.concatenate(
        [occ_beta, jnp.ones((1, tile_cols)), energy_beta[None, :], jnp.zeros((depth - orbitals - 2, tile_cols))],
        axis=0,
    )
    width = tile_cols // CHUNKS
    products = []
    for q in range(CHUNKS):
        gathered = lax.all_gather(coeff[:, q * width : (q + 1) * width], "row", axis=0, tiled=True)
        products.append(jnp.dot(masked, gathered, preferred_element_type=jnp.float32))
    update, sums = turn_and_finish(products, coeff, left, right, strings)
    correction = update * lax.rsqrt(sums[2] + 1e-06)
    stats = jnp.stack([sums[0], jnp.sqrt(sums[1])])
    return (correction, stats)


def solution(mesh):
    in_specs = (P("row", None), P("row", "col"), P("row", None), P(), P(), P())
    out_specs = (P("row", "col"), P())
    return jax.shard_map(body, mesh=mesh, in_specs=in_specs, out_specs=out_specs, check_vma=False)
```

```python
import functools
import math

import jax
import jax.numpy as jnp
from jax import lax
from jax.experimental import pallas as pl
from jax.experimental.layout import Layout, with_layout_constraint
from jax.experimental.pallas import tpu as pltpu
from jax.sharding import PartitionSpec as P

MESH = pl.DeviceIdType.MESH
HIGH = lax.Precision.HIGHEST


def turn_kernel(row_count, col_count, total, chunk, chunks, *refs):
    last = chunk == chunks - 1
    if last:
        products, arrived = refs[:chunks], refs[chunks : 2 * chunks - 1]
        c_ref, left_ref, right_ref, out_ref, stats_ref, recv = refs[2 * chunks - 1 : 2 * chunks + 5]
        refs = refs[2 * chunks + 5 :]
        mine, sums, sum_send, sum_recv = refs[-4:]
    else:
        products = refs[:1]
        recv = refs[1]
        refs = refs[2:]
    p_ref, packed, relay_a, relay_b, load_sem, own_send, recv_sem, arrive_a, arrive_b, send_a, send_b, self_sem = refs[:12]
    row = lax.axis_index("row")
    col = lax.axis_index("col")
    tile = p_ref.shape[0]
    half = tile // 2
    fold = row_count // col_count
    per = fold // chunks
    home = lax.div(row, fold)
    place = lax.rem(row, fold)
    turn = lax.div(place, chunks)
    count = row_count * col_count
    me = row * col_count + col
    is_home = home == col
    takes = lax.rem(place, chunks) == chunk
    if last:
        loads = [
            pltpu.make_async_copy(
                product.at[:, pl.ds(k * tile, tile)],
                p_ref.at[:, pl.ds((q + chunks * k) * tile, tile)],
                load_sem.at[q * per + k],
            )
            for q, product in enumerate(products)
            for k in range(per)
        ]
    else:
        loads = [pltpu.make_async_copy(products[0], p_ref, load_sem.at[0])]
    for load in loads:
        load.start()

    barrier = pltpu.get_barrier_semaphore()

    def greet(d, carry):
        other = lax.rem(me + d, count)
        pl.semaphore_signal(
            barrier,
            inc=1,
            device_id=(lax.div(other, col_count), lax.rem(other, col_count)),
            device_id_type=MESH,
        )
        return carry

    lax.fori_loop(1, count, greet, 0)
    pl.semaphore_wait(barrier, count - 1)
    for load in loads:
        load.wait()

    def columns(s):
        return pl.ds(pl.multiple_of(s * tile, tile), tile)

    def remote(src, dst, send, arrive, to_row, to_col):
        return pltpu.make_async_remote_copy(
            src_ref=src,
            dst_ref=dst,
            send_sem=send,
            recv_sem=arrive,
            device_id=(to_row, to_col),
            device_id_type=MESH,
        )

    def spot(k):
        kk = lax.rem(turn + k, per)
        return kk, chunk + chunks * kk

    def own_direct(k):
        kk, s = spot(k)
        near = col * fold + s
        return [
            remote(packed.at[kk, h], recv.at[place, h], own_send.at[kk, h], recv_sem.at[place, h], near, col)
            for h in range(2)
        ]

    def own_relayed(k):
        kk, s = spot(k)
        near = col * fold + s
        slot_a = col - (col > home).astype(jnp.int32)
        slot_b = row - fold * (home > col).astype(jnp.int32)
        return [
            remote(packed.at[kk, 0], relay_a.at[slot_a, kk], own_send.at[kk, 0], arrive_a.at[slot_a, kk], row, home),
            remote(packed.at[kk, 1], relay_b.at[slot_b], own_send.at[kk, 1], arrive_b.at[slot_b], near, col),
        ]

    def own_local():
        return [pltpu.make_async_copy(packed.at[turn, h], recv.at[place, h], self_sem.at[h]) for h in range(2)]

    def pack(k):
        kk, s = spot(k)
        cols = columns(s) if last else columns(kk)
        for h in range(2):
            peak = jnp.max(jnp.abs(p_ref[pl.ds(h * half, half), cols]), axis=0, keepdims=True)
            code = jnp.floor(jnp.log2(jnp.maximum(peak, 1e-30)) * 128.0) + 2.0
            grow = jnp.exp2(code * (-1.0 / 128.0)) * 32767.0
            packed[kk, h, pl.ds(half, 16)] = jnp.broadcast_to(code, (16, tile)).astype(jnp.int32).astype(jnp.int16)
            rows = min(64, half)
            for r in range(0, half, rows):
                value = p_ref[pl.ds(h * half + r, rows), cols] * grow
                packed[kk, h, pl.ds(r, rows)] = jnp.floor(value + 0.5).astype(jnp.int32).astype(jnp.int16)

    def exchange(phase, start):
        def one(d, carry):
            other = lax.rem(me + d, count)
            copy = remote(
                mine.at[phase],
                sums.at[phase, me],
                sum_send.at[phase, d],
                sum_recv.at[phase, me],
                lax.div(other, col_count),
                lax.rem(other, col_count),
            )
            if start:
                copy.start()
            else:
                copy.wait_send()
            return carry

        lax.fori_loop(1, count, one, 0)

    def gather_sums(phase):
        def one(d, carry):
            other = lax.rem(me + d, count)
            remote(
                mine.at[phase],
                sums.at[phase, other],
                sum_send.at[phase, d],
                sum_recv.at[phase, other],
                lax.div(other, col_count),
                lax.rem(other, col_count),
            ).wait_recv()
            return carry

        lax.fori_loop(1, count, one, 0)
        sums[phase, pl.ds(me, 1)] = mine[pl.ds(phase, 1)]
        every = jnp.sum(sums[phase], axis=0)
        return jnp.sum(every[0:8]), jnp.sum(every[8:16])

    def fold_sum(x):
        lanes = x.shape[1] // 128
        out = x[:, 0:128]
        for q in range(1, lanes):
            out = out + x[:, q * 128 : (q + 1) * 128]
        return jnp.sum(out.reshape(x.shape[0] // 8, 8, 128), axis=0)

    zero = jnp.zeros((8, 128), jnp.float32)
    if last:
        step_rows = min(32, tile)

        def early(r, carry):
            rows = pl.ds(pl.multiple_of(r * step_rows, step_rows), step_rows)
            c = c_ref[rows, :].astype(jnp.float32)
            return carry[0] + fold_sum(c * p_ref[rows, :]), carry[1] + fold_sum(c * c)

        proj, weight = lax.fori_loop(0, tile // step_rows, early, (zero, zero))
        mine[0, 0:8] = proj
        mine[0, 8:16] = weight
        exchange(0, True)

    def launch(k, carry):
        pack(k)

        @pl.when(jnp.logical_not(is_home))
        def _():
            for copy in own_relayed(k):
                copy.start()

        @pl.when(jnp.logical_and(is_home, jnp.logical_or(k > 0, jnp.logical_not(takes))))
        def _():
            for copy in own_direct(k):
                copy.start()

        return carry

    lax.fori_loop(0, per, launch, 0)

    @pl.when(jnp.logical_and(is_home, takes))
    def _():
        for copy in own_local():
            copy.start()
        for copy in own_local():
            copy.wait()

    def relay_first(t):
        slot = lax.div(t, per)
        group = slot + (slot >= col).astype(jnp.int32)
        kk, s = spot(lax.rem(t, per))
        return slot, kk, remote(
            relay_a.at[slot, kk], recv.at[place, 0], send_a.at[t], recv_sem.at[place, 0], group * fold + s, col
        )

    def relay_second(t):
        slot = lax.div(t, fold)
        group = slot + (slot >= col).astype(jnp.int32)
        far = lax.rem(place - lax.rem(t, fold) + fold, fold)
        slot_b = slot * fold + far
        return slot_b, remote(
            relay_b.at[slot_b], recv.at[far, 1], send_b.at[t], recv_sem.at[far, 1], row, group
        )

    @pl.when(is_home)
    def _():
        def step(t, carry):
            slot, kk, copy = relay_first(t)
            pltpu.make_async_copy(relay_a.at[slot, kk], relay_a.at[slot, kk], arrive_a.at[slot, kk]).wait()
            copy.start()
            return carry

        lax.fori_loop(0, (col_count - 1) * per, step, 0)

    @pl.when(jnp.logical_and(is_home, takes))
    def _():
        def step(t, carry):
            slot_b, copy = relay_second(t)
            pltpu.make_async_copy(relay_b.at[slot_b], relay_b.at[slot_b], arrive_b.at[slot_b]).wait()
            copy.start()
            return carry

        lax.fori_loop(0, (col_count - 1) * fold, step, 0)

    def await_piece(k):
        s = lax.rem(place - k + fold, fold)

        @pl.when(jnp.logical_and(takes, jnp.logical_not(jnp.logical_and(is_home, k == 0))))
        def _():
            for h in range(2):
                pltpu.make_async_copy(recv.at[s, h], recv.at[s, h], recv_sem.at[s, h]).wait()

    def settle():
        @pl.when(is_home)
        def _():
            def done(k, carry):
                @pl.when(jnp.logical_or(k > 0, jnp.logical_not(takes)))
                def _():
                    for copy in own_direct(k):
                        copy.wait_send()

                return carry

            lax.fori_loop(0, per, done, 0)

            def done_first(t, carry):
                relay_first(t)[-1].wait_send()
                return carry

            lax.fori_loop(0, (col_count - 1) * per, done_first, 0)

        @pl.when(jnp.logical_and(is_home, takes))
        def _():
            def done_second(t, carry):
                relay_second(t)[-1].wait_send()
                return carry

            lax.fori_loop(0, (col_count - 1) * fold, done_second, 0)

        @pl.when(jnp.logical_not(is_home))
        def _():
            def done(k, carry):
                for copy in own_relayed(k):
                    copy.wait_send()
                return carry

            lax.fori_loop(0, per, done, 0)

    if not last:

        def hold(k, carry):
            await_piece(k)
            return carry

        lax.fori_loop(0, fold, hold, 0)
        settle()
        return

    for q, ready in enumerate(arrived):

        @pl.when(lax.rem(place, chunks) == q)
        def _():
            fetch = pltpu.make_async_copy(ready, recv, self_sem.at[2])
            fetch.start()
            fetch.wait()

    proj, weight = gather_sums(0)
    theta = 2.0 * proj / weight

    piece = min(128, tile)

    def finish(k, carry):
        s = lax.rem(place - k + fold, fold)

        await_piece(k)

        def part(r, carry):
            squares, spread = carry
            rows = pl.ds(pl.multiple_of(r * piece, piece), piece)
            for h in range(2):
                cols = pl.ds(pl.multiple_of(s * tile + h * half, half), half)
                code = recv[s, h, pl.ds(half, 16), rows].astype(jnp.int32).astype(jnp.float32)[0:1]
                shrink = jnp.exp2(code * (1.0 / 128.0)) * (1.0 / 32767.0)
                value = recv[s, h, pl.ds(0, half), rows].astype(jnp.int32).astype(jnp.float32)
                turned = (value * shrink).T
                diagonal = jnp.dot(
                    left_ref[rows, :], right_ref[:, cols], precision=HIGH, preferred_element_type=jnp.float32
                )
                sigma = p_ref[rows, cols] + turned
                residual = sigma - theta * c_ref[rows, cols].astype(jnp.float32)
                update = residual / jnp.maximum(jnp.abs(diagonal - theta), 1.0)
                out_ref[rows, cols] = update
                squares = squares + fold_sum(residual * residual)
                spread = spread + fold_sum(update * update)
            return squares, spread

        return lax.fori_loop(0, tile // piece, part, carry)

    squares, spread = lax.fori_loop(0, fold, finish, (zero, zero))
    mine[1, 0:8] = squares
    mine[1, 8:16] = spread
    exchange(1, True)
    squares, spread = gather_sums(1)
    stats_ref[0] = theta
    stats_ref[1] = squares / total
    stats_ref[2] = spread / total

    exchange(0, False)
    exchange(1, False)
    settle()


def turn(chunk, chunks, products, arrived, coeff, left, right, strings):
    tile_rows, tile_cols = coeff.shape
    row_count = lax.axis_size("row")
    col_count = lax.axis_size("col")
    fold = row_count // col_count
    per = fold // chunks
    count = row_count * col_count
    tall = tile_rows // 2 + 16
    others = max(col_count - 1, 1)
    vmem = pl.BlockSpec(memory_space=pltpu.VMEM)
    anywhere = pl.BlockSpec(memory_space=pl.ANY)
    dma = pltpu.SemaphoreType.DMA
    last = chunk == chunks - 1
    arrival = (fold, 2, tall, tile_rows)
    scratch = [
        pltpu.VMEM((tile_rows, tile_cols if last else tile_cols // chunks), jnp.float32),
        pltpu.VMEM((per, 2, tall, tile_rows), jnp.int16),
        pltpu.VMEM((others, per, tall, tile_rows), jnp.int16),
        pltpu.VMEM((others * fold, tall, tile_rows), jnp.int16),
        dma((fold,)),
        dma((per, 2)),
        dma((fold, 2)),
        dma((others, per)),
        dma((others * fold,)),
        dma((others * per,)),
        dma((others * fold,)),
        dma((3,)),
    ]
    if last:
        operands = (*products, *arrived, coeff, left, right)
        in_specs = [anywhere] * (2 * chunks - 1) + [vmem] * 3
        out_shape = (
            jax.ShapeDtypeStruct((tile_rows, tile_cols), jnp.float32),
            jax.ShapeDtypeStruct((3,), jnp.float32),
        )
        out_specs = (vmem, pl.BlockSpec(memory_space=pltpu.SMEM))
        scratch = [
            pltpu.VMEM(arrival, jnp.int16),
            *scratch,
            pltpu.VMEM((2, 16, 128), jnp.float32),
            pltpu.VMEM((2, count, 16, 128), jnp.float32),
            dma((2, count)),
            dma((2, count)),
        ]
    else:
        operands = (products[chunk],)
        in_specs = [anywhere]
        out_shape = jax.ShapeDtypeStruct(arrival, jnp.int16)
        out_specs = vmem
    return pl.pallas_call(
        functools.partial(turn_kernel, row_count, col_count, float(strings) * float(strings), chunk, chunks),
        out_shape=out_shape,
        in_specs=in_specs,
        out_specs=out_specs,
        scratch_shapes=scratch,
        compiler_params=pltpu.CompilerParams(
            collective_id=chunk, has_side_effects=True, vmem_limit_bytes=(60 if last else 24) * 1024 * 1024
        ),
        name=f"turn_{chunk}",
    )(*operands)


CHUNKS = 4


def body(ham, coeff, tile_mask, occupation, orbital_energy, coulomb):
    tile_rows, strings = ham.shape
    tile_cols = coeff.shape[1]
    mask_cols = tile_mask.shape[1]
    block_size = strings // mask_cols
    mask_rows = tile_rows // block_size
    weights = tile_mask.astype(jnp.bfloat16)[:, None, :, None]
    masked = (ham.reshape(mask_rows, block_size, mask_cols, block_size) * weights).reshape(
        tile_rows, strings
    )
    occ_float = occupation.astype(jnp.float32)
    occ_alpha = lax.dynamic_slice_in_dim(occ_float, lax.axis_index("row") * tile_rows, tile_rows, 1)
    occ_beta = lax.dynamic_slice_in_dim(occ_float, lax.axis_index("col") * tile_cols, tile_cols, 1)
    energy_alpha = jnp.dot(orbital_energy, occ_alpha, precision=HIGH)
    energy_beta = jnp.dot(orbital_energy, occ_beta, precision=HIGH)
    mixed = jnp.dot(occ_alpha.T, coulomb, precision=HIGH)
    orbitals = occupation.shape[0]
    depth = -(-(orbitals + 2) // 128) * 128
    left = jnp.concatenate(
        [mixed, energy_alpha[:, None], jnp.ones((tile_rows, 1)), jnp.zeros((tile_rows, depth - orbitals - 2))],
        axis=1,
    )
    right = jnp.concatenate(
        [occ_beta, jnp.ones((1, tile_cols)), energy_beta[None, :], jnp.zeros((depth - orbitals - 2, tile_cols))],
        axis=0,
    )
    fold = tile_cols // tile_rows
    chunks = math.gcd(CHUNKS, fold)
    products = []
    arrived = []
    for q in range(chunks):
        part = jnp.concatenate(
            [coeff[:, s * tile_rows : (s + 1) * tile_rows] for s in range(q, fold, chunks)], axis=1
        )
        gathered = with_layout_constraint(lax.all_gather(part, "row", axis=0, tiled=True), Layout((0, 1)))
        products.append(jnp.dot(masked, gathered, preferred_element_type=jnp.float32))
        result = turn(q, chunks, products, arrived, coeff, left, right, strings)
        if q < chunks - 1:
            arrived.append(result)
    update, sums = result
    correction = update * lax.rsqrt(sums[2] + 1e-06)
    stats = jnp.stack([sums[0], jnp.sqrt(sums[1])])
    return (correction, stats)


def solution(mesh):
    in_specs = (P("row", None), P("row", "col"), P("row", None), P(), P(), P())
    out_specs = (P("row", "col"), P())
    return jax.shard_map(body, mesh=mesh, in_specs=in_specs, out_specs=out_specs, check_vma=False)
```

```python
import functools
import math

import jax
import jax.numpy as jnp
from jax import lax
from jax.experimental import pallas as pl
from jax.experimental.layout import Layout, with_layout_constraint
from jax.experimental.pallas import tpu as pltpu
from jax.sharding import PartitionSpec as P

MESH = pl.DeviceIdType.MESH
HIGH = lax.Precision.HIGHEST


def turn_kernel(row_count, col_count, total, chunk, chunks, *refs):
    last = chunk == chunks - 1
    if last:
        products, arrived = refs[:chunks], refs[chunks : 2 * chunks - 1]
        diagonal_ref, c_ref, out_ref, stats_ref, recv = refs[2 * chunks - 1 : 2 * chunks + 4]
        refs = refs[2 * chunks + 4 :]
        mine, sums, sum_send, sum_recv = refs[-4:]
    else:
        products = refs[:1]
        recv = refs[1]
        refs = refs[2:]
    p_ref, packed, relay_a, relay_b, load_sem, own_send, recv_sem, arrive_a, arrive_b, send_a, send_b, self_sem = refs[:12]
    row = lax.axis_index("row")
    col = lax.axis_index("col")
    tile = p_ref.shape[0]
    half = tile // 2
    fold = row_count // col_count
    per = fold // chunks
    home = lax.div(row, fold)
    place = lax.rem(row, fold)
    turn = lax.div(place, chunks)
    count = row_count * col_count
    me = row * col_count + col
    is_home = home == col
    takes = lax.rem(place, chunks) == chunk
    if last:
        loads = [
            pltpu.make_async_copy(
                product.at[:, pl.ds(k * tile, tile)],
                p_ref.at[:, pl.ds((q + chunks * k) * tile, tile)],
                load_sem.at[q * per + k],
            )
            for q, product in enumerate(products)
            for k in range(per)
        ]
    else:
        loads = [pltpu.make_async_copy(products[0], p_ref, load_sem.at[0])]
    for load in loads:
        load.start()
    if last:
        diagonal_load = pltpu.make_async_copy(diagonal_ref, out_ref, self_sem.at[3])
        diagonal_load.start()

    barrier = pltpu.get_barrier_semaphore()

    def greet(d, carry):
        other = lax.rem(me + d, count)
        pl.semaphore_signal(
            barrier,
            inc=1,
            device_id=(lax.div(other, col_count), lax.rem(other, col_count)),
            device_id_type=MESH,
        )
        return carry

    lax.fori_loop(1, count, greet, 0)
    pl.semaphore_wait(barrier, count - 1)
    for load in loads:
        load.wait()

    def columns(s):
        return pl.ds(pl.multiple_of(s * tile, tile), tile)

    def remote(src, dst, send, arrive, to_row, to_col):
        return pltpu.make_async_remote_copy(
            src_ref=src,
            dst_ref=dst,
            send_sem=send,
            recv_sem=arrive,
            device_id=(to_row, to_col),
            device_id_type=MESH,
        )

    def spot(k):
        kk = lax.rem(turn + k, per)
        return kk, chunk + chunks * kk

    def own_direct(k):
        kk, s = spot(k)
        near = col * fold + s
        return [
            remote(packed.at[kk, h], recv.at[place, h], own_send.at[kk, h], recv_sem.at[place, h], near, col)
            for h in range(2)
        ]

    def own_relayed(k):
        kk, s = spot(k)
        near = col * fold + s
        slot_a = col - (col > home).astype(jnp.int32)
        slot_b = row - fold * (home > col).astype(jnp.int32)
        return [
            remote(packed.at[kk, 0], relay_a.at[slot_a, kk], own_send.at[kk, 0], arrive_a.at[slot_a, kk], row, home),
            remote(packed.at[kk, 1], relay_b.at[slot_b], own_send.at[kk, 1], arrive_b.at[slot_b], near, col),
        ]

    def own_local():
        return [pltpu.make_async_copy(packed.at[turn, h], recv.at[place, h], self_sem.at[h]) for h in range(2)]

    def pack(k):
        kk, s = spot(k)
        cols = columns(s) if last else columns(kk)
        for h in range(2):
            peak = jnp.max(jnp.abs(p_ref[pl.ds(h * half, half), cols]), axis=0, keepdims=True)
            code = jnp.floor(jnp.log2(jnp.maximum(peak, 1e-30)) * 128.0) + 2.0
            grow = jnp.exp2(code * (-1.0 / 128.0)) * 32767.0
            packed[kk, h, pl.ds(half, 16)] = jnp.broadcast_to(code, (16, tile)).astype(jnp.int32).astype(jnp.int16)
            rows = min(64, half)
            for r in range(0, half, rows):
                value = p_ref[pl.ds(h * half + r, rows), cols] * grow
                packed[kk, h, pl.ds(r, rows)] = jnp.floor(value + 0.5).astype(jnp.int32).astype(jnp.int16)

    def exchange(phase, start):
        def one(d, carry):
            other = lax.rem(me + d, count)
            copy = remote(
                mine.at[phase],
                sums.at[phase, me],
                sum_send.at[phase, d],
                sum_recv.at[phase, me],
                lax.div(other, col_count),
                lax.rem(other, col_count),
            )
            if start:
                copy.start()
            else:
                copy.wait_send()
            return carry

        lax.fori_loop(1, count, one, 0)

    def gather_sums(phase):
        def one(d, carry):
            other = lax.rem(me + d, count)
            remote(
                mine.at[phase],
                sums.at[phase, other],
                sum_send.at[phase, d],
                sum_recv.at[phase, other],
                lax.div(other, col_count),
                lax.rem(other, col_count),
            ).wait_recv()
            return carry

        lax.fori_loop(1, count, one, 0)
        sums[phase, pl.ds(me, 1)] = mine[pl.ds(phase, 1)]
        every = jnp.sum(sums[phase], axis=0)
        return jnp.sum(every[0:8]), jnp.sum(every[8:16])

    def fold_sum(x):
        lanes = x.shape[1] // 128
        out = x[:, 0:128]
        for q in range(1, lanes):
            out = out + x[:, q * 128 : (q + 1) * 128]
        return jnp.sum(out.reshape(x.shape[0] // 8, 8, 128), axis=0)

    zero = jnp.zeros((8, 128), jnp.float32)
    if last:
        step_rows = min(32, tile)

        def early(r, carry):
            rows = pl.ds(pl.multiple_of(r * step_rows, step_rows), step_rows)
            c = c_ref[rows, :].astype(jnp.float32)
            return carry[0] + fold_sum(c * p_ref[rows, :]), carry[1] + fold_sum(c * c)

        proj, weight = lax.fori_loop(0, tile // step_rows, early, (zero, zero))
        mine[0, 0:8] = proj
        mine[0, 8:16] = weight
        exchange(0, True)

    def launch(k, carry):
        pack(k)

        @pl.when(jnp.logical_not(is_home))
        def _():
            for copy in own_relayed(k):
                copy.start()

        @pl.when(jnp.logical_and(is_home, jnp.logical_or(k > 0, jnp.logical_not(takes))))
        def _():
            for copy in own_direct(k):
                copy.start()

        return carry

    lax.fori_loop(0, per, launch, 0)

    @pl.when(jnp.logical_and(is_home, takes))
    def _():
        for copy in own_local():
            copy.start()
        for copy in own_local():
            copy.wait()

    def relay_first(t):
        slot = lax.div(t, per)
        group = slot + (slot >= col).astype(jnp.int32)
        kk, s = spot(lax.rem(t, per))
        return slot, kk, remote(
            relay_a.at[slot, kk], recv.at[place, 0], send_a.at[t], recv_sem.at[place, 0], group * fold + s, col
        )

    def relay_second(t):
        slot = lax.div(t, fold)
        group = slot + (slot >= col).astype(jnp.int32)
        far = lax.rem(place - lax.rem(t, fold) + fold, fold)
        slot_b = slot * fold + far
        return slot_b, remote(
            relay_b.at[slot_b], recv.at[far, 1], send_b.at[t], recv_sem.at[far, 1], row, group
        )

    @pl.when(is_home)
    def _():
        def step(t, carry):
            slot, kk, copy = relay_first(t)
            pltpu.make_async_copy(relay_a.at[slot, kk], relay_a.at[slot, kk], arrive_a.at[slot, kk]).wait()
            copy.start()
            return carry

        lax.fori_loop(0, (col_count - 1) * per, step, 0)

    @pl.when(jnp.logical_and(is_home, takes))
    def _():
        def step(t, carry):
            slot_b, copy = relay_second(t)
            pltpu.make_async_copy(relay_b.at[slot_b], relay_b.at[slot_b], arrive_b.at[slot_b]).wait()
            copy.start()
            return carry

        lax.fori_loop(0, (col_count - 1) * fold, step, 0)

    def await_piece(k):
        s = lax.rem(place - k + fold, fold)

        @pl.when(jnp.logical_and(takes, jnp.logical_not(jnp.logical_and(is_home, k == 0))))
        def _():
            for h in range(2):
                pltpu.make_async_copy(recv.at[s, h], recv.at[s, h], recv_sem.at[s, h]).wait()

    def settle():
        @pl.when(is_home)
        def _():
            def done(k, carry):
                @pl.when(jnp.logical_or(k > 0, jnp.logical_not(takes)))
                def _():
                    for copy in own_direct(k):
                        copy.wait_send()

                return carry

            lax.fori_loop(0, per, done, 0)

            def done_first(t, carry):
                relay_first(t)[-1].wait_send()
                return carry

            lax.fori_loop(0, (col_count - 1) * per, done_first, 0)

        @pl.when(jnp.logical_and(is_home, takes))
        def _():
            def done_second(t, carry):
                relay_second(t)[-1].wait_send()
                return carry

            lax.fori_loop(0, (col_count - 1) * fold, done_second, 0)

        @pl.when(jnp.logical_not(is_home))
        def _():
            def done(k, carry):
                for copy in own_relayed(k):
                    copy.wait_send()
                return carry

            lax.fori_loop(0, per, done, 0)

    if not last:

        def hold(k, carry):
            await_piece(k)
            return carry

        lax.fori_loop(0, fold, hold, 0)
        settle()
        return

    for q, ready in enumerate(arrived):

        @pl.when(lax.rem(place, chunks) == q)
        def _():
            fetch = pltpu.make_async_copy(ready, recv, self_sem.at[2])
            fetch.start()
            fetch.wait()

    proj, weight = gather_sums(0)
    theta = 2.0 * proj / weight
    diagonal_load.wait()

    piece = min(128, tile)

    def finish(k, carry):
        s = lax.rem(place - k + fold, fold)

        await_piece(k)

        def part(r, carry):
            squares, spread = carry
            rows = pl.ds(pl.multiple_of(r * piece, piece), piece)
            for h in range(2):
                cols = pl.ds(pl.multiple_of(s * tile + h * half, half), half)
                code = recv[s, h, pl.ds(half, 16), rows].astype(jnp.int32).astype(jnp.float32)[0:1]
                shrink = jnp.exp2(code * (1.0 / 128.0)) * (1.0 / 32767.0)
                value = recv[s, h, pl.ds(0, half), rows].astype(jnp.int32).astype(jnp.float32)
                turned = (value * shrink).T
                sigma = p_ref[rows, cols] + turned
                residual = sigma - theta * c_ref[rows, cols].astype(jnp.float32)
                update = residual / jnp.maximum(jnp.abs(out_ref[rows, cols] - theta), 1.0)
                out_ref[rows, cols] = update
                squares = squares + fold_sum(residual * residual)
                spread = spread + fold_sum(update * update)
            return squares, spread

        return lax.fori_loop(0, tile // piece, part, carry)

    squares, spread = lax.fori_loop(0, fold, finish, (zero, zero))
    mine[1, 0:8] = squares
    mine[1, 8:16] = spread
    exchange(1, True)
    squares, spread = gather_sums(1)
    stats_ref[0] = theta
    stats_ref[1] = squares / total
    stats_ref[2] = spread / total

    exchange(0, False)
    exchange(1, False)
    settle()


def turn(chunk, chunks, products, arrived, coeff, diagonal, strings):
    tile_rows, tile_cols = coeff.shape
    row_count = lax.axis_size("row")
    col_count = lax.axis_size("col")
    fold = row_count // col_count
    per = fold // chunks
    count = row_count * col_count
    tall = tile_rows // 2 + 16
    others = max(col_count - 1, 1)
    vmem = pl.BlockSpec(memory_space=pltpu.VMEM)
    anywhere = pl.BlockSpec(memory_space=pl.ANY)
    dma = pltpu.SemaphoreType.DMA
    last = chunk == chunks - 1
    arrival = (fold, 2, tall, tile_rows)
    scratch = [
        pltpu.VMEM((tile_rows, tile_cols if last else tile_cols // chunks), jnp.float32),
        pltpu.VMEM((per, 2, tall, tile_rows), jnp.int16),
        pltpu.VMEM((others, per, tall, tile_rows), jnp.int16),
        pltpu.VMEM((others * fold, tall, tile_rows), jnp.int16),
        dma((fold,)),
        dma((per, 2)),
        dma((fold, 2)),
        dma((others, per)),
        dma((others * fold,)),
        dma((others * per,)),
        dma((others * fold,)),
        dma((4,)),
    ]
    if last:
        operands = (*products, *arrived, diagonal, coeff)
        in_specs = [anywhere] * (2 * chunks) + [vmem]
        out_shape = (
            jax.ShapeDtypeStruct((tile_rows, tile_cols), jnp.float32),
            jax.ShapeDtypeStruct((3,), jnp.float32),
        )
        out_specs = (vmem, pl.BlockSpec(memory_space=pltpu.SMEM))
        scratch = [
            pltpu.VMEM(arrival, jnp.int16),
            *scratch,
            pltpu.VMEM((2, 16, 128), jnp.float32),
            pltpu.VMEM((2, count, 16, 128), jnp.float32),
            dma((2, count)),
            dma((2, count)),
        ]
    else:
        operands = (products[chunk],)
        in_specs = [anywhere]
        out_shape = jax.ShapeDtypeStruct(arrival, jnp.int16)
        out_specs = vmem
    return pl.pallas_call(
        functools.partial(turn_kernel, row_count, col_count, float(strings) * float(strings), chunk, chunks),
        out_shape=out_shape,
        in_specs=in_specs,
        out_specs=out_specs,
        scratch_shapes=scratch,
        compiler_params=pltpu.CompilerParams(
            collective_id=chunk, has_side_effects=True, vmem_limit_bytes=(60 if last else 24) * 1024 * 1024
        ),
        name=f"turn_{chunk}",
    )(*operands)


CHUNKS = 2


def body(ham, coeff, tile_mask, occupation, orbital_energy, coulomb):
    tile_rows, strings = ham.shape
    tile_cols = coeff.shape[1]
    mask_cols = tile_mask.shape[1]
    block_size = strings // mask_cols
    mask_rows = tile_rows // block_size
    weights = tile_mask.astype(jnp.bfloat16)[:, None, :, None]
    masked = (ham.reshape(mask_rows, block_size, mask_cols, block_size) * weights).reshape(
        tile_rows, strings
    )
    occ_float = occupation.astype(jnp.float32)
    occ_alpha = lax.dynamic_slice_in_dim(occ_float, lax.axis_index("row") * tile_rows, tile_rows, 1)
    occ_beta = lax.dynamic_slice_in_dim(occ_float, lax.axis_index("col") * tile_cols, tile_cols, 1)
    energy_alpha = jnp.dot(orbital_energy, occ_alpha, precision=HIGH)
    energy_beta = jnp.dot(orbital_energy, occ_beta, precision=HIGH)
    coupling = jnp.dot(jnp.dot(occ_alpha.T, coulomb, precision=HIGH), occ_beta, precision=HIGH)
    diagonal = energy_alpha[:, None] + energy_beta[None, :] + coupling
    fold = tile_cols // tile_rows
    chunks = math.gcd(CHUNKS, fold)
    products = []
    arrived = []
    for q in range(chunks):
        part = jnp.concatenate(
            [coeff[:, s * tile_rows : (s + 1) * tile_rows] for s in range(q, fold, chunks)], axis=1
        )
        gathered = with_layout_constraint(lax.all_gather(part, "row", axis=0, tiled=True), Layout((0, 1)))
        products.append(jnp.dot(masked, gathered, preferred_element_type=jnp.float32))
        result = turn(q, chunks, products, arrived, coeff, diagonal, strings)
        if q < chunks - 1:
            arrived.append(result)
    update, sums = result
    correction = update * lax.rsqrt(sums[2] + 1e-06)
    stats = jnp.stack([sums[0], jnp.sqrt(sums[1])])
    return (correction, stats)


def solution(mesh):
    in_specs = (P("row", None), P("row", "col"), P("row", None), P(), P(), P())
    out_specs = (P("row", "col"), P())
    return jax.shard_map(body, mesh=mesh, in_specs=in_specs, out_specs=out_specs, check_vma=False)
```

```python
import functools

import jax
import jax.numpy as jnp
from jax import lax
from jax.experimental import pallas as pl
from jax.experimental.layout import Layout, with_layout_constraint
from jax.experimental.pallas import tpu as pltpu
from jax.sharding import PartitionSpec as P

MESH = pl.DeviceIdType.MESH
HIGH = lax.Precision.HIGHEST
STRIDE = 4


def members(chunk, chunks, fold):
    return [s for s in range(fold) if (s % STRIDE == STRIDE - 1) == (chunk == chunks - 1)]


def turn_kernel(row_count, col_count, total, chunk, chunks, *refs):
    last = chunk == chunks - 1
    if last:
        products, arrived = refs[:chunks], refs[chunks : 2 * chunks - 1]
        diagonal_ref, c_ref, out_ref, stats_ref, recv = refs[2 * chunks - 1 : 2 * chunks + 4]
        refs = refs[2 * chunks + 4 :]
        mine, sums, sum_send, sum_recv = refs[-4:]
    else:
        products = refs[:1]
        recv = refs[1]
        refs = refs[2:]
    p_ref, packed, relay_a, relay_b, load_sem, own_send, recv_sem, arrive_a, arrive_b, send_a, send_b, self_sem = refs[:12]
    row = lax.axis_index("row")
    col = lax.axis_index("col")
    tile = p_ref.shape[0]
    half = tile // 2
    fold = row_count // col_count
    per = len(members(chunk, chunks, fold))
    home = lax.div(row, fold)
    place = lax.rem(row, fold)
    turn = lax.div(place, STRIDE)
    if not last:
        turn = lax.rem(turn * (STRIDE - 1) + lax.rem(place, STRIDE), per)
    count = row_count * col_count
    me = row * col_count + col
    is_home = home == col
    takes = (lax.rem(place, STRIDE) == STRIDE - 1) if last else (lax.rem(place, STRIDE) < STRIDE - 1)
    if last:
        loads = [
            pltpu.make_async_copy(
                product.at[:, pl.ds(k * tile, tile)],
                p_ref.at[:, pl.ds(s * tile, tile)],
                load_sem.at[s],
            )
            for q, product in enumerate(products)
            for k, s in enumerate(members(q, chunks, fold))
        ]
    else:
        loads = [pltpu.make_async_copy(products[0], p_ref, load_sem.at[0])]
    for load in loads:
        load.start()
    if last:
        diagonal_load = pltpu.make_async_copy(diagonal_ref, out_ref, self_sem.at[3])
        diagonal_load.start()

    barrier = pltpu.get_barrier_semaphore()

    def greet(d, carry):
        other = lax.rem(me + d, count)
        pl.semaphore_signal(
            barrier,
            inc=1,
            device_id=(lax.div(other, col_count), lax.rem(other, col_count)),
            device_id_type=MESH,
        )
        return carry

    lax.fori_loop(1, count, greet, 0)
    pl.semaphore_wait(barrier, count - 1)
    for load in loads:
        load.wait()

    def columns(s):
        return pl.ds(pl.multiple_of(s * tile, tile), tile)

    def remote(src, dst, send, arrive, to_row, to_col):
        return pltpu.make_async_remote_copy(
            src_ref=src,
            dst_ref=dst,
            send_sem=send,
            recv_sem=arrive,
            device_id=(to_row, to_col),
            device_id_type=MESH,
        )

    def spot(k):
        kk = lax.rem(turn + k, per)
        if last:
            return kk, kk * STRIDE + STRIDE - 1
        return kk, lax.div(kk, STRIDE - 1) * STRIDE + lax.rem(kk, STRIDE - 1)

    def own_direct(k):
        kk, s = spot(k)
        near = col * fold + s
        return [
            remote(packed.at[kk, h], recv.at[place, h], own_send.at[kk, h], recv_sem.at[place, h], near, col)
            for h in range(2)
        ]

    def own_relayed(k):
        kk, s = spot(k)
        near = col * fold + s
        slot_a = col - (col > home).astype(jnp.int32)
        slot_b = row - fold * (home > col).astype(jnp.int32)
        return [
            remote(packed.at[kk, 0], relay_a.at[slot_a, kk], own_send.at[kk, 0], arrive_a.at[slot_a, kk], row, home),
            remote(packed.at[kk, 1], relay_b.at[slot_b], own_send.at[kk, 1], arrive_b.at[slot_b], near, col),
        ]

    def own_local():
        return [pltpu.make_async_copy(packed.at[turn, h], recv.at[place, h], self_sem.at[h]) for h in range(2)]

    def pack(k):
        kk, s = spot(k)
        cols = columns(s) if last else columns(kk)
        for h in range(2):
            peak = jnp.max(jnp.abs(p_ref[pl.ds(h * half, half), cols]), axis=0, keepdims=True)
            code = jnp.floor(jnp.log2(jnp.maximum(peak, 1e-30)) * 128.0) + 2.0
            grow = jnp.exp2(code * (-1.0 / 128.0)) * 32767.0
            packed[kk, h, pl.ds(half, 16)] = jnp.broadcast_to(code, (16, tile)).astype(jnp.int32).astype(jnp.int16)
            rows = min(64, half)
            for r in range(0, half, rows):
                value = p_ref[pl.ds(h * half + r, rows), cols] * grow
                packed[kk, h, pl.ds(r, rows)] = jnp.floor(value + 0.5).astype(jnp.int32).astype(jnp.int16)

    def exchange(phase, start):
        def one(d, carry):
            other = lax.rem(me + d, count)
            copy = remote(
                mine.at[phase],
                sums.at[phase, me],
                sum_send.at[phase, d],
                sum_recv.at[phase, me],
                lax.div(other, col_count),
                lax.rem(other, col_count),
            )
            if start:
                copy.start()
            else:
                copy.wait_send()
            return carry

        lax.fori_loop(1, count, one, 0)

    def gather_sums(phase):
        def one(d, carry):
            other = lax.rem(me + d, count)
            remote(
                mine.at[phase],
                sums.at[phase, other],
                sum_send.at[phase, d],
                sum_recv.at[phase, other],
                lax.div(other, col_count),
                lax.rem(other, col_count),
            ).wait_recv()
            return carry

        lax.fori_loop(1, count, one, 0)
        sums[phase, pl.ds(me, 1)] = mine[pl.ds(phase, 1)]
        every = jnp.sum(sums[phase], axis=0)
        return jnp.sum(every[0:8]), jnp.sum(every[8:16])

    def fold_sum(x):
        lanes = x.shape[1] // 128
        out = x[:, 0:128]
        for q in range(1, lanes):
            out = out + x[:, q * 128 : (q + 1) * 128]
        return jnp.sum(out.reshape(x.shape[0] // 8, 8, 128), axis=0)

    zero = jnp.zeros((8, 128), jnp.float32)
    if last:
        step_rows = min(32, tile)

        def early(r, carry):
            rows = pl.ds(pl.multiple_of(r * step_rows, step_rows), step_rows)
            c = c_ref[rows, :].astype(jnp.float32)
            return carry[0] + fold_sum(c * p_ref[rows, :]), carry[1] + fold_sum(c * c)

        proj, weight = lax.fori_loop(0, tile // step_rows, early, (zero, zero))
        mine[0, 0:8] = proj
        mine[0, 8:16] = weight
        exchange(0, True)

    def launch(k, carry):
        pack(k)

        @pl.when(jnp.logical_not(is_home))
        def _():
            for copy in own_relayed(k):
                copy.start()

        @pl.when(jnp.logical_and(is_home, jnp.logical_or(k > 0, jnp.logical_not(takes))))
        def _():
            for copy in own_direct(k):
                copy.start()

        return carry

    lax.fori_loop(0, per, launch, 0)

    @pl.when(jnp.logical_and(is_home, takes))
    def _():
        for copy in own_local():
            copy.start()
        for copy in own_local():
            copy.wait()

    def relay_first(t):
        slot = lax.div(t, per)
        group = slot + (slot >= col).astype(jnp.int32)
        kk, s = spot(lax.rem(t, per))
        return slot, kk, remote(
            relay_a.at[slot, kk], recv.at[place, 0], send_a.at[t], recv_sem.at[place, 0], group * fold + s, col
        )

    def relay_second(t):
        slot = lax.div(t, fold)
        group = slot + (slot >= col).astype(jnp.int32)
        far = lax.rem(place - lax.rem(t, fold) + fold, fold)
        slot_b = slot * fold + far
        return slot_b, remote(
            relay_b.at[slot_b], recv.at[far, 1], send_b.at[t], recv_sem.at[far, 1], row, group
        )

    @pl.when(is_home)
    def _():
        def step(t, carry):
            slot, kk, copy = relay_first(t)
            pltpu.make_async_copy(relay_a.at[slot, kk], relay_a.at[slot, kk], arrive_a.at[slot, kk]).wait()
            copy.start()
            return carry

        lax.fori_loop(0, (col_count - 1) * per, step, 0)

    @pl.when(jnp.logical_and(is_home, takes))
    def _():
        def step(t, carry):
            slot_b, copy = relay_second(t)
            pltpu.make_async_copy(relay_b.at[slot_b], relay_b.at[slot_b], arrive_b.at[slot_b]).wait()
            copy.start()
            return carry

        lax.fori_loop(0, (col_count - 1) * fold, step, 0)

    def await_piece(k):
        s = lax.rem(place - k + fold, fold)

        @pl.when(jnp.logical_and(takes, jnp.logical_not(jnp.logical_and(is_home, k == 0))))
        def _():
            for h in range(2):
                pltpu.make_async_copy(recv.at[s, h], recv.at[s, h], recv_sem.at[s, h]).wait()

    def settle():
        @pl.when(is_home)
        def _():
            def done(k, carry):
                @pl.when(jnp.logical_or(k > 0, jnp.logical_not(takes)))
                def _():
                    for copy in own_direct(k):
                        copy.wait_send()

                return carry

            lax.fori_loop(0, per, done, 0)

            def done_first(t, carry):
                relay_first(t)[-1].wait_send()
                return carry

            lax.fori_loop(0, (col_count - 1) * per, done_first, 0)

        @pl.when(jnp.logical_and(is_home, takes))
        def _():
            def done_second(t, carry):
                relay_second(t)[-1].wait_send()
                return carry

            lax.fori_loop(0, (col_count - 1) * fold, done_second, 0)

        @pl.when(jnp.logical_not(is_home))
        def _():
            def done(k, carry):
                for copy in own_relayed(k):
                    copy.wait_send()
                return carry

            lax.fori_loop(0, per, done, 0)

    if not last:

        def hold(k, carry):
            await_piece(k)
            return carry

        lax.fori_loop(0, fold, hold, 0)
        settle()
        return

    for ready in arrived:

        @pl.when(jnp.logical_not(takes))
        def _():
            fetch = pltpu.make_async_copy(ready, recv, self_sem.at[2])
            fetch.start()
            fetch.wait()

    proj, weight = gather_sums(0)
    theta = 2.0 * proj / weight
    diagonal_load.wait()

    piece = min(128, tile)

    def finish(k, carry):
        s = lax.rem(place - k + fold, fold)

        await_piece(k)

        def part(r, carry):
            squares, spread = carry
            rows = pl.ds(pl.multiple_of(r * piece, piece), piece)
            for h in range(2):
                cols = pl.ds(pl.multiple_of(s * tile + h * half, half), half)
                code = recv[s, h, pl.ds(half, 16), rows].astype(jnp.int32).astype(jnp.float32)[0:1]
                shrink = jnp.exp2(code * (1.0 / 128.0)) * (1.0 / 32767.0)
                value = recv[s, h, pl.ds(0, half), rows].astype(jnp.int32).astype(jnp.float32)
                turned = (value * shrink).T
                sigma = p_ref[rows, cols] + turned
                residual = sigma - theta * c_ref[rows, cols].astype(jnp.float32)
                update = residual / jnp.maximum(jnp.abs(out_ref[rows, cols] - theta), 1.0)
                out_ref[rows, cols] = update
                squares = squares + fold_sum(residual * residual)
                spread = spread + fold_sum(update * update)
            return squares, spread

        return lax.fori_loop(0, tile // piece, part, carry)

    squares, spread = lax.fori_loop(0, fold, finish, (zero, zero))
    mine[1, 0:8] = squares
    mine[1, 8:16] = spread
    exchange(1, True)
    squares, spread = gather_sums(1)
    stats_ref[0] = theta
    stats_ref[1] = squares / total
    stats_ref[2] = spread / total

    exchange(0, False)
    exchange(1, False)
    settle()


def turn(chunk, chunks, products, arrived, coeff, diagonal, strings):
    tile_rows, tile_cols = coeff.shape
    row_count = lax.axis_size("row")
    col_count = lax.axis_size("col")
    fold = row_count // col_count
    per = len(members(chunk, chunks, fold))
    count = row_count * col_count
    tall = tile_rows // 2 + 16
    others = max(col_count - 1, 1)
    vmem = pl.BlockSpec(memory_space=pltpu.VMEM)
    anywhere = pl.BlockSpec(memory_space=pl.ANY)
    dma = pltpu.SemaphoreType.DMA
    last = chunk == chunks - 1
    arrival = (fold, 2, tall, tile_rows)
    scratch = [
        pltpu.VMEM((tile_rows, tile_cols if last else per * tile_rows), jnp.float32),
        pltpu.VMEM((per, 2, tall, tile_rows), jnp.int16),
        pltpu.VMEM((others, per, tall, tile_rows), jnp.int16),
        pltpu.VMEM((others * fold, tall, tile_rows), jnp.int16),
        dma((fold,)),
        dma((per, 2)),
        dma((fold, 2)),
        dma((others, per)),
        dma((others * fold,)),
        dma((others * per,)),
        dma((others * fold,)),
        dma((4,)),
    ]
    if last:
        operands = (*products, *arrived, diagonal, coeff)
        in_specs = [anywhere] * (2 * chunks) + [vmem]
        out_shape = (
            jax.ShapeDtypeStruct((tile_rows, tile_cols), jnp.float32),
            jax.ShapeDtypeStruct((3,), jnp.float32),
        )
        out_specs = (vmem, pl.BlockSpec(memory_space=pltpu.SMEM))
        scratch = [
            pltpu.VMEM(arrival, jnp.int16),
            *scratch,
            pltpu.VMEM((2, 16, 128), jnp.float32),
            pltpu.VMEM((2, count, 16, 128), jnp.float32),
            dma((2, count)),
            dma((2, count)),
        ]
    else:
        operands = (products[chunk],)
        in_specs = [anywhere]
        out_shape = jax.ShapeDtypeStruct(arrival, jnp.int16)
        out_specs = vmem
    return pl.pallas_call(
        functools.partial(turn_kernel, row_count, col_count, float(strings) * float(strings), chunk, chunks),
        out_shape=out_shape,
        in_specs=in_specs,
        out_specs=out_specs,
        scratch_shapes=scratch,
        compiler_params=pltpu.CompilerParams(
            collective_id=chunk, has_side_effects=True, vmem_limit_bytes=(60 if last else 24) * 1024 * 1024
        ),
        name=f"turn_{chunk}",
    )(*operands)


def body(ham, coeff, tile_mask, occupation, orbital_energy, coulomb):
    tile_rows, strings = ham.shape
    tile_cols = coeff.shape[1]
    mask_cols = tile_mask.shape[1]
    block_size = strings // mask_cols
    mask_rows = tile_rows // block_size
    weights = tile_mask.astype(jnp.bfloat16)[:, None, :, None]
    masked = (ham.reshape(mask_rows, block_size, mask_cols, block_size) * weights).reshape(
        tile_rows, strings
    )
    occ_float = occupation.astype(jnp.float32)
    occ_alpha = lax.dynamic_slice_in_dim(occ_float, lax.axis_index("row") * tile_rows, tile_rows, 1)
    occ_beta = lax.dynamic_slice_in_dim(occ_float, lax.axis_index("col") * tile_cols, tile_cols, 1)
    energy_alpha = jnp.dot(orbital_energy, occ_alpha, precision=HIGH)
    energy_beta = jnp.dot(orbital_energy, occ_beta, precision=HIGH)
    coupling = jnp.dot(jnp.dot(occ_alpha.T, coulomb, precision=HIGH), occ_beta, precision=HIGH)
    diagonal = energy_alpha[:, None] + energy_beta[None, :] + coupling
    fold = tile_cols // tile_rows
    chunks = 2
    products = []
    arrived = []
    for q in range(chunks):
        part = jnp.concatenate(
            [coeff[:, s * tile_rows : (s + 1) * tile_rows] for s in members(q, chunks, fold)], axis=1
        )
        gathered = with_layout_constraint(lax.all_gather(part, "row", axis=0, tiled=True), Layout((0, 1)))
        products.append(jnp.dot(masked, gathered, preferred_element_type=jnp.float32))
        result = turn(q, chunks, products, arrived, coeff, diagonal, strings)
        if q < chunks - 1:
            arrived.append(result)
    update, sums = result
    correction = update * lax.rsqrt(sums[2] + 1e-06)
    stats = jnp.stack([sums[0], jnp.sqrt(sums[1])])
    return (correction, stats)


def solution(mesh):
    in_specs = (P("row", None), P("row", "col"), P("row", None), P(), P(), P())
    out_specs = (P("row", "col"), P())
    return jax.shard_map(body, mesh=mesh, in_specs=in_specs, out_specs=out_specs, check_vma=False)
```

```python
import functools

import jax
import jax.numpy as jnp
from jax import lax
from jax.experimental import pallas as pl
from jax.experimental.layout import Layout, with_layout_constraint
from jax.experimental.pallas import tpu as pltpu
from jax.sharding import PartitionSpec as P

MESH = pl.DeviceIdType.MESH
HIGH = lax.Precision.HIGHEST
STRIDE = 4


def members(chunk, chunks, fold):
    return [s for s in range(fold) if (s % STRIDE == STRIDE - 1) == (chunk == chunks - 1)]


def turn_kernel(row_count, col_count, total, chunk, chunks, *refs):
    last = chunk == chunks - 1
    if last:
        products, arrived = refs[:chunks], refs[chunks : 2 * chunks - 1]
        diagonal_ref, c_ref, out_ref, stats_ref, recv = refs[2 * chunks - 1 : 2 * chunks + 4]
        refs = refs[2 * chunks + 4 :]
        mine, sums, sum_send, sum_recv = refs[-4:]
    else:
        products = refs[:1]
        recv = refs[1]
        refs = refs[2:]
    p_ref, packed, relay_a, relay_b, load_sem, own_send, recv_sem, arrive_a, arrive_b, send_a, send_b, self_sem = refs[:12]
    row = lax.axis_index("row")
    col = lax.axis_index("col")
    tile = p_ref.shape[0]
    half = tile // 2
    fold = row_count // col_count
    per = len(members(chunk, chunks, fold))
    home = lax.div(row, fold)
    place = lax.rem(row, fold)
    turn = lax.div(place, STRIDE)
    if not last:
        turn = lax.rem(turn * (STRIDE - 1) + lax.rem(place, STRIDE), per)
    count = row_count * col_count
    me = row * col_count + col
    is_home = home == col
    takes = (lax.rem(place, STRIDE) == STRIDE - 1) if last else (lax.rem(place, STRIDE) < STRIDE - 1)
    if last:
        loads = [
            pltpu.make_async_copy(
                product.at[:, pl.ds(k * tile, tile)],
                p_ref.at[:, pl.ds(s * tile, tile)],
                load_sem.at[s],
            )
            for q, product in enumerate(products)
            for k, s in enumerate(members(q, chunks, fold))
        ]
    else:
        loads = [pltpu.make_async_copy(products[0], p_ref, load_sem.at[0])]
    for load in loads:
        load.start()
    if last:
        diagonal_load = pltpu.make_async_copy(diagonal_ref, out_ref, self_sem.at[3])
        diagonal_load.start()

    barrier = pltpu.get_barrier_semaphore()

    def greet(d, carry):
        other = lax.rem(me + d, count)
        pl.semaphore_signal(
            barrier,
            inc=1,
            device_id=(lax.div(other, col_count), lax.rem(other, col_count)),
            device_id_type=MESH,
        )
        return carry

    lax.fori_loop(1, count, greet, 0)
    pl.semaphore_wait(barrier, count - 1)
    for load in loads:
        load.wait()

    def columns(s):
        return pl.ds(pl.multiple_of(s * tile, tile), tile)

    def remote(src, dst, send, arrive, to_row, to_col):
        return pltpu.make_async_remote_copy(
            src_ref=src,
            dst_ref=dst,
            send_sem=send,
            recv_sem=arrive,
            device_id=(to_row, to_col),
            device_id_type=MESH,
        )

    def spot(k):
        kk = lax.rem(turn + k, per)
        if last:
            return kk, kk * STRIDE + STRIDE - 1
        return kk, lax.div(kk, STRIDE - 1) * STRIDE + lax.rem(kk, STRIDE - 1)

    def own_direct(k):
        kk, s = spot(k)
        near = col * fold + s
        return [
            remote(packed.at[kk, h], recv.at[place, h], own_send.at[kk, h], recv_sem.at[place, h], near, col)
            for h in range(2)
        ]

    def own_relayed(k):
        kk, s = spot(k)
        near = col * fold + s
        slot_a = col - (col > home).astype(jnp.int32)
        slot_b = row - fold * (home > col).astype(jnp.int32)
        return [
            remote(packed.at[kk, 0], relay_a.at[slot_a, kk], own_send.at[kk, 0], arrive_a.at[slot_a, kk], row, home),
            remote(packed.at[kk, 1], relay_b.at[slot_b], own_send.at[kk, 1], arrive_b.at[slot_b], near, col),
        ]

    def own_local():
        return [pltpu.make_async_copy(packed.at[turn, h], recv.at[place, h], self_sem.at[h]) for h in range(2)]

    def pack(k):
        kk, s = spot(k)
        cols = columns(s) if last else columns(kk)
        for h in range(2):
            peak = jnp.max(jnp.abs(p_ref[pl.ds(h * half, half), cols]), axis=0, keepdims=True)
            code = jnp.floor(jnp.log2(jnp.maximum(peak, 1e-30)) * 128.0) + 2.0
            grow = jnp.exp2(code * (-1.0 / 128.0)) * 32767.0
            packed[kk, h, pl.ds(half, 16)] = jnp.broadcast_to(code, (16, tile)).astype(jnp.int32).astype(jnp.int16)
            rows = min(64, half)
            for r in range(0, half, rows):
                value = p_ref[pl.ds(h * half + r, rows), cols] * grow
                packed[kk, h, pl.ds(r, rows)] = jnp.floor(value + 0.5).astype(jnp.int32).astype(jnp.int16)

    def exchange(phase, start):
        def one(d, carry):
            other = lax.rem(me + d, count)
            copy = remote(
                mine.at[phase],
                sums.at[phase, me],
                sum_send.at[phase, d],
                sum_recv.at[phase, me],
                lax.div(other, col_count),
                lax.rem(other, col_count),
            )
            if start:
                copy.start()
            else:
                copy.wait_send()
            return carry

        lax.fori_loop(1, count, one, 0)

    def gather_sums(phase):
        def one(d, carry):
            other = lax.rem(me + d, count)
            remote(
                mine.at[phase],
                sums.at[phase, other],
                sum_send.at[phase, d],
                sum_recv.at[phase, other],
                lax.div(other, col_count),
                lax.rem(other, col_count),
            ).wait_recv()
            return carry

        lax.fori_loop(1, count, one, 0)
        sums[phase, pl.ds(me, 1)] = mine[pl.ds(phase, 1)]
        every = jnp.sum(sums[phase], axis=0)
        return jnp.sum(every[0:8]), jnp.sum(every[8:16])

    def fold_sum(x):
        lanes = x.shape[1] // 128
        out = x[:, 0:128]
        for q in range(1, lanes):
            out = out + x[:, q * 128 : (q + 1) * 128]
        return jnp.sum(out.reshape(x.shape[0] // 8, 8, 128), axis=0)

    zero = jnp.zeros((8, 128), jnp.float32)
    if last:
        step_rows = min(32, tile)

        def early(r, carry):
            rows = pl.ds(pl.multiple_of(r * step_rows, step_rows), step_rows)
            c = c_ref[rows, :].astype(jnp.float32)
            return carry[0] + fold_sum(c * p_ref[rows, :]), carry[1] + fold_sum(c * c)

        proj, weight = lax.fori_loop(0, tile // step_rows, early, (zero, zero))
        mine[0, 0:8] = proj
        mine[0, 8:16] = weight
        exchange(0, True)

    def launch(k, carry):
        pack(k)

        @pl.when(jnp.logical_not(is_home))
        def _():
            for copy in own_relayed(k):
                copy.start()

        @pl.when(jnp.logical_and(is_home, jnp.logical_or(k > 0, jnp.logical_not(takes))))
        def _():
            for copy in own_direct(k):
                copy.start()

        return carry

    lax.fori_loop(0, per, launch, 0)

    @pl.when(jnp.logical_and(is_home, takes))
    def _():
        for copy in own_local():
            copy.start()
        for copy in own_local():
            copy.wait()

    def relay_first(t):
        slot = lax.div(t, per)
        group = slot + (slot >= col).astype(jnp.int32)
        kk, s = spot(lax.rem(t, per))
        return slot, kk, remote(
            relay_a.at[slot, kk], recv.at[place, 0], send_a.at[t], recv_sem.at[place, 0], group * fold + s, col
        )

    def relay_second(t):
        slot = lax.div(t, fold)
        group = slot + (slot >= col).astype(jnp.int32)
        far = lax.rem(place - lax.rem(t, fold) + fold, fold)
        slot_b = slot * fold + far
        return slot_b, remote(
            relay_b.at[slot_b], recv.at[far, 1], send_b.at[t], recv_sem.at[far, 1], row, group
        )

    @pl.when(is_home)
    def _():
        def step(t, carry):
            slot, kk, copy = relay_first(t)
            pltpu.make_async_copy(relay_a.at[slot, kk], relay_a.at[slot, kk], arrive_a.at[slot, kk]).wait()
            copy.start()
            return carry

        lax.fori_loop(0, (col_count - 1) * per, step, 0)

    @pl.when(jnp.logical_and(is_home, takes))
    def _():
        def step(t, carry):
            slot_b, copy = relay_second(t)
            pltpu.make_async_copy(relay_b.at[slot_b], relay_b.at[slot_b], arrive_b.at[slot_b]).wait()
            copy.start()
            return carry

        lax.fori_loop(0, (col_count - 1) * fold, step, 0)

    def await_piece(k):
        s = lax.rem(place - k + fold, fold)

        @pl.when(jnp.logical_and(takes, jnp.logical_not(jnp.logical_and(is_home, k == 0))))
        def _():
            for h in range(2):
                pltpu.make_async_copy(recv.at[s, h], recv.at[s, h], recv_sem.at[s, h]).wait()

    def settle():
        @pl.when(is_home)
        def _():
            def done(k, carry):
                @pl.when(jnp.logical_or(k > 0, jnp.logical_not(takes)))
                def _():
                    for copy in own_direct(k):
                        copy.wait_send()

                return carry

            lax.fori_loop(0, per, done, 0)

            def done_first(t, carry):
                relay_first(t)[-1].wait_send()
                return carry

            lax.fori_loop(0, (col_count - 1) * per, done_first, 0)

        @pl.when(jnp.logical_and(is_home, takes))
        def _():
            def done_second(t, carry):
                relay_second(t)[-1].wait_send()
                return carry

            lax.fori_loop(0, (col_count - 1) * fold, done_second, 0)

        @pl.when(jnp.logical_not(is_home))
        def _():
            def done(k, carry):
                for copy in own_relayed(k):
                    copy.wait_send()
                return carry

            lax.fori_loop(0, per, done, 0)

    if not last:

        def hold(k, carry):
            await_piece(k)
            return carry

        lax.fori_loop(0, fold, hold, 0)
        settle()
        return

    for ready in arrived:

        @pl.when(jnp.logical_not(takes))
        def _():
            fetch = pltpu.make_async_copy(ready, recv, self_sem.at[2])
            fetch.start()
            fetch.wait()

    proj, weight = gather_sums(0)
    theta = 2.0 * proj / weight
    diagonal_load.wait()

    piece = min(128, tile)

    def finish(k, carry):
        s = lax.rem(place - k + fold, fold)

        await_piece(k)

        def part(r, carry):
            squares, spread = carry
            rows = pl.ds(pl.multiple_of(r * piece, piece), piece)
            for h in range(2):
                cols = pl.ds(pl.multiple_of(s * tile + h * half, half), half)
                code = recv[s, h, pl.ds(half, 16), rows].astype(jnp.int32).astype(jnp.float32)[0:1]
                shrink = jnp.exp2(code * (1.0 / 128.0)) * (1.0 / 32767.0)
                value = recv[s, h, pl.ds(0, half), rows].astype(jnp.int32).astype(jnp.float32)
                turned = (value * shrink).T
                sigma = p_ref[rows, cols] + turned
                residual = sigma - theta * c_ref[rows, cols].astype(jnp.float32)
                update = residual / jnp.maximum(jnp.abs(out_ref[rows, cols] - theta), 1.0)
                out_ref[rows, cols] = update
                squares = squares + fold_sum(residual * residual)
                spread = spread + fold_sum(update * update)
            return squares, spread

        return lax.fori_loop(0, tile // piece, part, carry)

    squares, spread = lax.fori_loop(0, fold, finish, (zero, zero))
    mine[1, 0:8] = squares
    mine[1, 8:16] = spread
    exchange(1, True)
    squares, spread = gather_sums(1)
    stats_ref[0] = theta
    stats_ref[1] = squares / total
    stats_ref[2] = spread / total

    exchange(0, False)
    exchange(1, False)
    settle()


def turn(chunk, chunks, products, arrived, coeff, diagonal, strings):
    tile_rows, tile_cols = coeff.shape
    row_count = lax.axis_size("row")
    col_count = lax.axis_size("col")
    fold = row_count // col_count
    per = len(members(chunk, chunks, fold))
    count = row_count * col_count
    tall = tile_rows // 2 + 16
    others = max(col_count - 1, 1)
    vmem = pl.BlockSpec(memory_space=pltpu.VMEM)
    anywhere = pl.BlockSpec(memory_space=pl.ANY)
    dma = pltpu.SemaphoreType.DMA
    last = chunk == chunks - 1
    arrival = (fold, 2, tall, tile_rows)
    scratch = [
        pltpu.VMEM((tile_rows, tile_cols if last else per * tile_rows), jnp.float32),
        pltpu.VMEM((per, 2, tall, tile_rows), jnp.int16),
        pltpu.VMEM((others, per, tall, tile_rows), jnp.int16),
        pltpu.VMEM((others * fold, tall, tile_rows), jnp.int16),
        dma((fold,)),
        dma((per, 2)),
        dma((fold, 2)),
        dma((others, per)),
        dma((others * fold,)),
        dma((others * per,)),
        dma((others * fold,)),
        dma((4,)),
    ]
    if last:
        operands = (*products, *arrived, diagonal, coeff)
        in_specs = [anywhere] * (2 * chunks) + [vmem]
        out_shape = (
            jax.ShapeDtypeStruct((tile_rows, tile_cols), jnp.float32),
            jax.ShapeDtypeStruct((3,), jnp.float32),
        )
        out_specs = (vmem, pl.BlockSpec(memory_space=pltpu.SMEM))
        scratch = [
            pltpu.VMEM(arrival, jnp.int16),
            *scratch,
            pltpu.VMEM((2, 16, 128), jnp.float32),
            pltpu.VMEM((2, count, 16, 128), jnp.float32),
            dma((2, count)),
            dma((2, count)),
        ]
    else:
        operands = (products[chunk],)
        in_specs = [anywhere]
        out_shape = jax.ShapeDtypeStruct(arrival, jnp.int16)
        out_specs = vmem
    return pl.pallas_call(
        functools.partial(turn_kernel, row_count, col_count, float(strings) * float(strings), chunk, chunks),
        out_shape=out_shape,
        in_specs=in_specs,
        out_specs=out_specs,
        scratch_shapes=scratch,
        compiler_params=pltpu.CompilerParams(
            collective_id=chunk, has_side_effects=True, vmem_limit_bytes=(60 if last else 24) * 1024 * 1024
        ),
        name=f"turn_{chunk}",
    )(*operands)


def body(ham, coeff, tile_mask, occupation, orbital_energy, coulomb):
    tile_rows, strings = ham.shape
    tile_cols = coeff.shape[1]
    mask_cols = tile_mask.shape[1]
    block_size = strings // mask_cols
    mask_rows = tile_rows // block_size
    weights = tile_mask.astype(jnp.bfloat16)[:, None, :, None]
    masked = (ham.reshape(mask_rows, block_size, mask_cols, block_size) * weights).reshape(
        tile_rows, strings
    )
    occ_float = occupation.astype(jnp.float32)
    occ_alpha = lax.dynamic_slice_in_dim(occ_float, lax.axis_index("row") * tile_rows, tile_rows, 1)
    occ_beta = lax.dynamic_slice_in_dim(occ_float, lax.axis_index("col") * tile_cols, tile_cols, 1)
    energy_alpha = jnp.dot(orbital_energy, occ_alpha, precision=HIGH)
    energy_beta = jnp.dot(orbital_energy, occ_beta, precision=HIGH)
    coupling = jnp.dot(jnp.dot(occ_alpha.T, coulomb, precision=HIGH), occ_beta, precision=HIGH)
    diagonal = energy_alpha[:, None] + energy_beta[None, :] + coupling
    fold = tile_cols // tile_rows
    chunks = 2
    products = []
    arrived = []
    for q in range(chunks):
        part = jnp.concatenate(
            [coeff[:, s * tile_rows : (s + 1) * tile_rows] for s in members(q, chunks, fold)], axis=1
        )
        if q > 0:
            part, gathered = lax.optimization_barrier((part, gathered))
        gathered = with_layout_constraint(lax.all_gather(part, "row", axis=0, tiled=True), Layout((0, 1)))
        products.append(jnp.dot(masked, gathered, preferred_element_type=jnp.float32))
        result = turn(q, chunks, products, arrived, coeff, diagonal, strings)
        if q < chunks - 1:
            arrived.append(result)
    update, sums = result
    correction = update * lax.rsqrt(sums[2] + 1e-06)
    stats = jnp.stack([sums[0], jnp.sqrt(sums[1])])
    return (correction, stats)


def solution(mesh):
    in_specs = (P("row", None), P("row", "col"), P("row", None), P(), P(), P())
    out_specs = (P("row", "col"), P())
    return jax.shard_map(body, mesh=mesh, in_specs=in_specs, out_specs=out_specs, check_vma=False)
```
